32 devices in a mesh: runs: 2 (over x), sec: 16 (over z, y, core).
Axes of the slice: x: 2, y: 2, z: 4, core: 2. Of those that a mesh axis runs over, the one named last changes fastest.
Arguments:
- edge_rows: bfloat16 [4096, 1024], P(('runs', 'sec')), parts along dimension 0, may hold values from -46 to 46
- corner: bfloat16 [32768, 1024], P(('runs', 'sec')), parts along dimension 0, may hold values from -1 to 2.2
- joining: int32 [32, 16], P('runs'), parts along dimension 0, may hold values from 0 to 15, as said below
- charge_left: int32 [4096], P(('runs', 'sec')), parts along dimension 0, may hold values from 0 to 15
- charge_right: int32 [4096], P(('runs', 'sec')), parts along dimension 0, may hold values from 0 to 15
Outputs:
- isometry: float32 [4096, 1024], P(('runs', 'sec')), parts along dimension 0
The draws below stay inside these ranges and needn't reach their ends.
There are 2 independent parts, one for each index of `runs`. The reference program is written for one: setup_inputs(seed, part) draws one part's arguments, and reference() takes and returns one part's arrays. A program takes and returns all parts, laid end to end along the dimension named above; each array names one. Nothing has to cross between parts.
Inputs may be any that keep to these rules, and one draw needn't show every extreme that they name: joining[charge_left[e], charge_right[e]] names the block that row e needs; each row of joining names every block once; among the 128 rows of one device at most 16 need the same block, and one block, drawn per copy, receives exactly 16 rows from every device.
All inputs are finite; a program needn't handle non-finite values.
Results may differ from the reference program's by a relative error of at most 0.0003.
Values may be sent and summed in bfloat16 or wider, within the bound.
A program may use at most 128 MiB of HBM per device.

```python
import math
import jax
import jax.numpy as jnp
from jax import lax

W = 1024
ROWS = 128
BLOCKS = 16
CAP = 16
EDGES = 2048


def route_plan(key):
    perm = jax.random.permutation(jax.random.fold_in(key, 11), BLOCKS).astype(jnp.int32)
    hot_block = jax.random.randint(jax.random.fold_in(key, 12), (), 0, BLOCKS)
    popular = jax.random.randint(jax.random.fold_in(key, 13), (BLOCKS,), 0, 1 << 14)
    slots = BLOCKS * CAP
    slot_block = jnp.arange(slots, dtype=jnp.int32) // CAP

    def one_source(source):
        source_key = jax.random.fold_in(jax.random.fold_in(key, 14), source)
        noise = jax.random.randint(source_key, (slots,), 0, 1 << 14)
        score = (noise + popular[slot_block]) * 4096 + jnp.arange(slots, dtype=jnp.int32)
        score = score + jnp.where(slot_block == hot_block, 1 << 29, 0)
        chosen = lax.top_k(score, ROWS)[1]
        chosen = jax.random.permutation(jax.random.fold_in(source_key, 1), chosen)
        return slot_block[chosen]
    target = jax.vmap(one_source)(jnp.arange(BLOCKS, dtype=jnp.int32)).reshape(-1)
    left = jax.random.randint(jax.random.fold_in(key, 15), (EDGES,), 0, BLOCKS)
    inverse = jnp.argsort(perm).astype(jnp.int32)
    right = (inverse[target] - left) % BLOCKS
    grid_a = jnp.arange(BLOCKS, dtype=jnp.int32)[:, None]
    grid_b = jnp.arange(BLOCKS, dtype=jnp.int32)[None, :]
    table = perm[(grid_a + grid_b) % BLOCKS]
    return (table, left, right)


def draw_joining(key, part):
    return route_plan(key)[0]


def draw_charge_left(key, part):
    return route_plan(key)[1]


def draw_charge_right(key, part):
    return route_plan(key)[2]


def draw_edge_rows(key, part):
    position = jnp.arange(EDGES, dtype=jnp.float32)[:, None] / EDGES
    rising = jnp.exp(math.log(3.0) * position)
    row_scale = jnp.exp(jax.random.uniform(jax.random.fold_in(key, 2), (EDGES, 1), minval=math.log(0.3), maxval=math.log(3.0)))
    base = jnp.clip(jax.random.normal(jax.random.fold_in(key, 1), (EDGES, W)), -5.0, 5.0)
    return (base * row_scale * rising).astype(jnp.bfloat16)


def draw_corner(key, part):
    row_index = jnp.arange(BLOCKS * W, dtype=jnp.int32)[:, None] % W
    col_index = jnp.arange(W, dtype=jnp.int32)[None, :]
    on_diag = row_index == col_index
    diag_value = jnp.exp(jax.random.uniform(jax.random.fold_in(key, 1), (BLOCKS * W, W), minval=0.0, maxval=math.log(2.0)))
    spread = jnp.clip(jax.random.normal(jax.random.fold_in(key, 2), (BLOCKS * W, W)), -5.0, 5.0)
    off_value = spread * (0.5 / math.sqrt(W))
    return jnp.where(on_diag, diag_value, off_value).astype(jnp.bfloat16)


def setup_inputs(seed: int = 0, part: int = 0) -> dict:
    keys = jax.random.split(jax.random.key(seed), 6)
    part_keys = jax.random.split(jax.random.fold_in(keys[5], part), 6)
    return {
        "edge_rows": draw_edge_rows(jax.random.fold_in(jax.random.fold_in(keys[5], part), 71), part),
        "corner": draw_corner(jax.random.fold_in(jax.random.fold_in(keys[5], part), 71), part),
        "joining": draw_joining(jax.random.fold_in(jax.random.fold_in(keys[5], part), 71), part),
        "charge_left": draw_charge_left(jax.random.fold_in(jax.random.fold_in(keys[5], part), 71), part),
        "charge_right": draw_charge_right(jax.random.fold_in(jax.random.fold_in(keys[5], part), 71), part),
    }


def reference(edge_rows, corner, joining, charge_left, charge_right):
    target = joining[charge_left, charge_right]
    count = BLOCKS * CAP

    def one_block(carry, block):
        picked = jnp.nonzero(target == block, size=count, fill_value=EDGES)[0]
        taken = jnp.take(edge_rows, picked, axis=0, mode='fill', fill_value=0).astype(jnp.float32)
        weight = lax.dynamic_slice_in_dim(corner, (block * W).astype(jnp.int32), W, 0).astype(jnp.float32)
        image = jnp.dot(taken, weight, precision=lax.Precision.HIGHEST)
        carry = carry.at[picked].set(image, mode='drop')
        return (carry, None)
    images, _ = lax.scan(one_block, jnp.zeros((EDGES, W), jnp.float32), jnp.arange(BLOCKS, dtype=jnp.int32))
    gram = lax.dot_general(images, images, (((0,), (0,)), ((), ())), precision=lax.Precision.HIGHEST)
    lower = jnp.linalg.cholesky(gram)
    solved = lax.linalg.triangular_solve(lower, images, left_side=False, lower=True, transpose_a=True)
    return solved * math.sqrt(EDGES)
```

```python
import math

import jax
import jax.numpy as jnp
from jax import lax
from jax.experimental import pallas as pl
from jax.experimental.pallas import tpu as pltpu
from jax.sharding import PartitionSpec as P

B = 128
S = 8
F32 = jnp.float32
BF16 = jnp.bfloat16


def split2(x):
    hi = x.astype(BF16)
    lo = (x - hi.astype(F32)).astype(BF16)
    return hi, lo


def starts(nb):
    offs, at = [], 0
    for j in range(nb):
        offs.append(at)
        at += (nb - j) * B
    return offs, at


def dot(a, b, dims):
    return lax.dot_general(a, b, (dims, ((), ())), preferred_element_type=F32)


def product_kernel(nb, rows_ref, corner_ref, image_ref, gram_ref):
    image = dot(rows_ref[...], corner_ref[...], ((1,), (0,)))
    image_ref[...] = image
    hi, lo = split2(image)
    left = jnp.concatenate([hi, hi, lo], axis=0).T
    right = jnp.concatenate([hi, lo, hi], axis=0)
    offs, _ = starts(nb)
    for j in range(nb):
        gram_ref[pl.ds(offs[j], (nb - j) * B), :] = dot(
            left[j * B :, :], right[:, j * B : (j + 1) * B], ((1,), (0,))
        )


def factor_block(t_ref):
    row8 = lax.broadcasted_iota(jnp.int32, (S, B), 0)
    lane = lax.broadcasted_iota(jnp.int32, (S, B), 1)
    rowb = lax.broadcasted_iota(jnp.int32, (B, 2 * B), 0)

    def step(i, carry):
        at = pl.multiple_of(i * S, S)
        v0 = t_ref[pl.ds(at, S), :B]
        v1 = t_ref[pl.ds(at, S), B:]
        turned = pltpu.roll(v0, lax.rem(B - at, B), 1)
        cols = [jnp.broadcast_to(turned[:, m : m + 1], (S, B)) for m in range(S)]
        scale = jnp.zeros((S, B), F32)
        for j in range(S):
            pivot = cols[j][j : j + 1, :]
            f = jnp.where(row8 > j, cols[j] * (1.0 / pivot), 0.0)
            scale = jnp.where(row8 == j, lax.rsqrt(pivot), scale)
            for m in range(j + 1, S):
                cols[m] = cols[m] - f * cols[m][j : j + 1, :]
            v0 = v0 - f * v0[j : j + 1, :]
            v1 = v1 - f * v1[j : j + 1, :]
        v0 = v0 * scale
        v1 = v1 * scale
        u = jnp.where(lane >= at + S, v0, 0.0)
        uh = u.astype(BF16).astype(F32)
        um = (u - uh).astype(BF16).astype(F32)
        ul = u - uh - um
        v = jnp.concatenate([v0, v1], axis=1)
        vh = v.astype(BF16).astype(F32)
        vm = (v - vh).astype(BF16).astype(F32)
        vl = v - vh - vm
        lhs = jnp.concatenate([uh, uh, um, um, uh, ul], axis=0).astype(BF16)
        rhs = jnp.concatenate([vh, vm, vh, vm, vl, vh], axis=0).astype(BF16)
        change = dot(lhs, rhs, ((0,), (0,)))
        t_ref[...] = t_ref[...] - change
        t_ref[pl.ds(at, S), B:] = v1
        return carry

    lax.fori_loop(0, B // S, step, 0)


def solve_kernel(nb, factor, gram_ref, home_ref, out_ref, a_ref, t_ref):
    offs, total = starts(nb)
    rows = home_ref.shape[0]
    a_ref[...] = gram_ref[...]
    out_ref[...] = home_ref[...]
    eye = (
        lax.broadcasted_iota(jnp.int32, (B, B), 0) == lax.broadcasted_iota(jnp.int32, (B, B), 1)
    ).astype(F32)
    for k in range(nb):
        t_ref[:, :B] = a_ref[pl.ds(offs[k], B), :]
        t_ref[:, B:] = eye
        factor_block(t_ref)
        ih, il = split2(t_ref[:, B:])
        inv = jnp.concatenate([ih, il, ih], axis=1)
        below = (nb - k - 1) * B
        x = out_ref[:, k * B : (k + 1) * B]
        if below:
            x = jnp.concatenate([a_ref[pl.ds(offs[k] + B, below), :], x], axis=0)
        xh, xl = split2(x)
        panel = dot(jnp.concatenate([xh, xh, xl], axis=1), inv, ((1,), (1,)))
        out_ref[:, k * B : (k + 1) * B] = panel[below:, :] * factor
        if below:
            ph, plo = split2(panel)
            left = jnp.concatenate([ph, ph, plo], axis=1)
            right = jnp.concatenate([ph, plo, ph], axis=1)
            for j in range(k + 1, nb):
                at = (j - k - 1) * B
                change = dot(left[at:, :], right[at : at + B, :], ((1,), (1,)))
                size = (nb - j) * B
                a_ref[pl.ds(offs[j], size), :] = a_ref[pl.ds(offs[j], size), :] - change[:size, :]
                out_ref[:, j * B : (j + 1) * B] = (
                    out_ref[:, j * B : (j + 1) * B] - change[size:, :]
                )


def products(rows, corner):
    nb = corner.shape[1] // B
    _, total = starts(nb)
    vmem = pl.BlockSpec(memory_space=pltpu.VMEM)
    return pl.pallas_call(
        lambda *refs: product_kernel(nb, *refs),
        out_shape=(
            jax.ShapeDtypeStruct((rows.shape[0], corner.shape[1]), F32),
            jax.ShapeDtypeStruct((total, B), F32),
        ),
        in_specs=[vmem, vmem],
        out_specs=(vmem, vmem),
        compiler_params=pltpu.CompilerParams(vmem_limit_bytes=48 << 20),
        name="products",
    )(rows, corner)


def solve_rows(gram, home, factor):
    nb = home.shape[1] // B
    vmem = pl.BlockSpec(memory_space=pltpu.VMEM)
    return pl.pallas_call(
        lambda *refs: solve_kernel(nb, factor, *refs),
        out_shape=jax.ShapeDtypeStruct(home.shape, F32),
        in_specs=[vmem, vmem],
        out_specs=vmem,
        scratch_shapes=[pltpu.VMEM(gram.shape, F32), pltpu.VMEM((B, 2 * B), F32)],
        compiler_params=pltpu.CompilerParams(vmem_limit_bytes=48 << 20),
        name="solve_rows",
    )(gram, home)


def per_device(edge_rows, corner, joining, charge_left, charge_right):
    row_count, feature_len = edge_rows.shape
    owners = lax.axis_size("sec")
    capacity = 2 * row_count // owners
    factor = math.sqrt(row_count * owners)
    target = joining[charge_left, charge_right]
    labels = jnp.arange(owners, dtype=jnp.int32)
    onehot = (target[:, None] == labels[None, :]).astype(jnp.int32)
    before = jnp.cumsum(onehot, axis=0) - onehot
    order_in = jnp.sum(before * onehot, axis=1)
    slot_index = target * capacity + order_in
    packed = (
        jnp.zeros((owners * capacity, feature_len), edge_rows.dtype).at[slot_index].set(edge_rows)
    )
    arrived = lax.all_to_all(
        packed.reshape(owners, capacity, feature_len),
        "sec",
        split_axis=0,
        concat_axis=0,
        tiled=True,
    )
    product, gram_part = products(arrived.reshape(owners * capacity, feature_len), corner)
    gram = lax.psum(gram_part, "sec")
    returned = lax.all_to_all(
        product.reshape(owners, capacity, feature_len),
        "sec",
        split_axis=0,
        concat_axis=0,
        tiled=True,
    )
    home_rows = returned.reshape(owners * capacity, feature_len)[slot_index]
    return solve_rows(gram, home_rows, factor)


def solution(mesh):
    placed = (
        P(("runs", "sec"), None),
        P(("runs", "sec"), None),
        P("runs", None),
        P(("runs", "sec")),
        P(("runs", "sec")),
    )
    return jax.shard_map(
        per_device, mesh=mesh, in_specs=placed, out_specs=P(("runs", "sec"), None), check_vma=False
    )
```

```python
import math

import jax
import jax.numpy as jnp
from jax import lax
from jax.experimental import pallas as pl
from jax.experimental.pallas import tpu as pltpu
from jax.sharding import PartitionSpec as P

B = 128
S = 8
F32 = jnp.float32
BF16 = jnp.bfloat16


def split2(x):
    hi = x.astype(BF16)
    lo = (x - hi.astype(F32)).astype(BF16)
    return hi, lo


def starts(nb):
    offs, at = [], 0
    for j in range(nb):
        offs.append(at)
        at += (nb - j) * B
    return offs, at


def dot(a, b, dims):
    return lax.dot_general(a, b, (dims, ((), ())), preferred_element_type=F32)


def product_kernel(nb, rows_ref, corner_ref, image_ref, gram_ref):
    image = dot(rows_ref[...], corner_ref[...], ((1,), (0,)))
    image_ref[...] = image
    hi, lo = split2(image)
    left = jnp.concatenate([hi, hi, lo], axis=0).T
    right = jnp.concatenate([hi, lo, hi], axis=0)
    offs, _ = starts(nb)
    for j in range(nb):
        gram_ref[pl.ds(offs[j], (nb - j) * B), :] = dot(
            left[j * B :, :], right[:, j * B : (j + 1) * B], ((1,), (0,))
        )


def factor_block(t_ref):
    row8 = lax.broadcasted_iota(jnp.int32, (S, B), 0)
    lane = lax.broadcasted_iota(jnp.int32, (S, B), 1)
    rowb = lax.broadcasted_iota(jnp.int32, (B, 2 * B), 0)

    def step(i, carry):
        at = pl.multiple_of(i * S, S)
        v0 = t_ref[pl.ds(at, S), :B]
        v1 = t_ref[pl.ds(at, S), B:]
        turned = pltpu.roll(v0, lax.rem(B - at, B), 1)
        cols = [jnp.broadcast_to(turned[:, m : m + 1], (S, B)) for m in range(S)]
        scale = jnp.zeros((S, B), F32)
        for j in range(S):
            pivot = cols[j][j : j + 1, :]
            f = jnp.where(row8 > j, cols[j] * (1.0 / pivot), 0.0)
            scale = jnp.where(row8 == j, lax.rsqrt(pivot), scale)
            for m in range(j + 1, S):
                cols[m] = cols[m] - f * cols[m][j : j + 1, :]
            v0 = v0 - f * v0[j : j + 1, :]
            v1 = v1 - f * v1[j : j + 1, :]
        v0 = v0 * scale
        v1 = v1 * scale
        u = jnp.where(lane >= at + S, v0, 0.0)
        uh = u.astype(BF16).astype(F32)
        um = (u - uh).astype(BF16).astype(F32)
        ul = u - uh - um
        v = jnp.concatenate([v0, v1], axis=1)
        vh = v.astype(BF16).astype(F32)
        vm = (v - vh).astype(BF16).astype(F32)
        vl = v - vh - vm
        lhs = jnp.concatenate([uh, uh, um, um, uh, ul], axis=0).astype(BF16)
        rhs = jnp.concatenate([vh, vm, vh, vm, vl, vh], axis=0).astype(BF16)
        change = dot(lhs, rhs, ((0,), (0,)))
        t_ref[...] = t_ref[...] - change
        t_ref[pl.ds(at, S), B:] = v1
        return carry

    lax.fori_loop(0, B // S, step, 0)


def solve_kernel(nb, factor, gram_ref, home_ref, out_ref, a_ref, t_ref):
    offs, total = starts(nb)
    rows = home_ref.shape[0]
    a_ref[...] = gram_ref[...]
    out_ref[...] = home_ref[...]
    eye = (
        lax.broadcasted_iota(jnp.int32, (B, B), 0) == lax.broadcasted_iota(jnp.int32, (B, B), 1)
    ).astype(F32)
    for k in range(nb):
        t_ref[:, :B] = a_ref[pl.ds(offs[k], B), :]
        t_ref[:, B:] = eye
        factor_block(t_ref)
        ih, il = split2(t_ref[:, B:])
        inv = jnp.concatenate([ih, il, ih], axis=1)
        below = (nb - k - 1) * B
        x = out_ref[:, k * B : (k + 1) * B]
        if below:
            x = jnp.concatenate([a_ref[pl.ds(offs[k] + B, below), :], x], axis=0)
        xh, xl = split2(x)
        panel = dot(jnp.concatenate([xh, xh, xl], axis=1), inv, ((1,), (1,)))
        out_ref[:, k * B : (k + 1) * B] = panel[below:, :] * factor
        if below:
            ph, plo = split2(panel)
            left = jnp.concatenate([ph, ph, plo], axis=1)
            right = jnp.concatenate([ph, plo, ph], axis=1)
            for j in range(k + 1, nb):
                at = (j - k - 1) * B
                change = dot(left[at:, :], right[at : at + B, :], ((1,), (1,)))
                size = (nb - j) * B
                a_ref[pl.ds(offs[j], size), :] = a_ref[pl.ds(offs[j], size), :] - change[:size, :]
                out_ref[:, j * B : (j + 1) * B] = (
                    out_ref[:, j * B : (j + 1) * B] - change[size:, :]
                )


def total_kernel(stages, chunks, part_ref, out_ref, acc_ref, inbox_ref, send_sem, recv_sem):
    me = lax.axis_index("sec")
    rows = part_ref.shape[0] // chunks
    bit = [(me // (1 << s)) % 2 for s in range(stages)]
    peer = [me + (1 << s) * (1 - 2 * bit[s]) for s in range(stages)]
    barrier = pltpu.get_barrier_semaphore()
    for s in range(stages):
        pl.semaphore_signal(
            barrier, inc=1, device_id={"sec": peer[s]}, device_id_type=pl.DeviceIdType.MESH
        )
    pl.semaphore_wait(barrier, stages)

    base = [[None] * (stages + 1) for _ in range(chunks)]
    for c in range(chunks):
        base[c][0] = c * rows
        for s in range(stages):
            base[c][s + 1] = base[c][s] + bit[s] * (rows >> (s + 1))

    def window(c, s, flip):
        size = rows >> (s + 1)
        side = 1 - bit[s] if flip else bit[s]
        return pl.ds(pl.multiple_of(base[c][s] + side * size, 8), size)

    def box(c, s):
        return pl.ds(c * rows + rows - (rows >> s), rows >> (s + 1))

    def make(c, t):
        if t < stages:
            source = part_ref if t == 0 else acc_ref
            src = source.at[window(c, t, True), :]
            dst = inbox_ref.at[box(c, t), :]
            s = t
        else:
            s = 2 * stages - 1 - t
            src = out_ref.at[window(c, s, False), :]
            dst = out_ref.at[window(c, s, False), :]
        return pltpu.make_async_remote_copy(
            src_ref=src,
            dst_ref=dst,
            send_sem=send_sem.at[c, t],
            recv_sem=recv_sem.at[c, t],
            device_id={"sec": peer[s]},
            device_id_type=pl.DeviceIdType.MESH,
        )

    copies = {}
    for step in range(2 * stages + chunks):
        for c in range(chunks):
            t = step - c
            if t < 0 or t > 2 * stages:
                continue
            if t > 0:
                copies[c, t - 1].wait()
                if t <= stages:
                    mine = window(c, t - 1, False)
                    source = part_ref if t == 1 else acc_ref
                    result = out_ref if t == stages else acc_ref
                    result[mine, :] = source[mine, :] + inbox_ref[box(c, t - 1), :]
            if t < 2 * stages:
                copies[c, t] = make(c, t)
                copies[c, t].start()


def total_over_sec(part, owners):
    stages = owners.bit_length() - 1
    grain = 8 * owners
    chunks = 4 if part.shape[0] % (4 * grain) == 0 else 1
    rows = -(-part.shape[0] // grain) * grain
    padded = jnp.pad(part, ((0, rows - part.shape[0]), (0, 0)))
    vmem = pl.BlockSpec(memory_space=pltpu.VMEM)
    total = pl.pallas_call(
        lambda *refs: total_kernel(stages, chunks, *refs),
        out_shape=jax.ShapeDtypeStruct((rows, B), F32),
        in_specs=[vmem],
        out_specs=vmem,
        scratch_shapes=[
            pltpu.VMEM((rows, B), F32),
            pltpu.VMEM((rows, B), F32),
            pltpu.SemaphoreType.DMA((chunks, 2 * stages)),
            pltpu.SemaphoreType.DMA((chunks, 2 * stages)),
        ],
        compiler_params=pltpu.CompilerParams(
            collective_id=0, has_side_effects=True, vmem_limit_bytes=40 << 20
        ),
        name="total_over_sec",
    )(padded)
    return total[: part.shape[0]]


def products(rows, corner):
    nb = corner.shape[1] // B
    _, total = starts(nb)
    vmem = pl.BlockSpec(memory_space=pltpu.VMEM)
    return pl.pallas_call(
        lambda *refs: product_kernel(nb, *refs),
        out_shape=(
            jax.ShapeDtypeStruct((rows.shape[0], corner.shape[1]), F32),
            jax.ShapeDtypeStruct((total, B), F32),
        ),
        in_specs=[vmem, vmem],
        out_specs=(vmem, vmem),
        compiler_params=pltpu.CompilerParams(vmem_limit_bytes=48 << 20),
        name="products",
    )(rows, corner)


def solve_rows(gram, home, factor):
    nb = home.shape[1] // B
    vmem = pl.BlockSpec(memory_space=pltpu.VMEM)
    return pl.pallas_call(
        lambda *refs: solve_kernel(nb, factor, *refs),
        out_shape=jax.ShapeDtypeStruct(home.shape, F32),
        in_specs=[vmem, vmem],
        out_specs=vmem,
        scratch_shapes=[pltpu.VMEM(gram.shape, F32), pltpu.VMEM((B, 2 * B), F32)],
        compiler_params=pltpu.CompilerParams(vmem_limit_bytes=48 << 20),
        name="solve_rows",
    )(gram, home)


def per_device(edge_rows, corner, joining, charge_left, charge_right):
    row_count, feature_len = edge_rows.shape
    owners = lax.axis_size("sec")
    capacity = 2 * row_count // owners
    factor = math.sqrt(row_count * owners)
    target = joining[charge_left, charge_right]
    labels = jnp.arange(owners, dtype=jnp.int32)
    onehot = (target[:, None] == labels[None, :]).astype(jnp.int32)
    before = jnp.cumsum(onehot, axis=0) - onehot
    order_in = jnp.sum(before * onehot, axis=1)
    slot_index = target * capacity + order_in
    packed = (
        jnp.zeros((owners * capacity, feature_len), edge_rows.dtype).at[slot_index].set(edge_rows)
    )
    arrived = lax.all_to_all(
        packed.reshape(owners, capacity, feature_len),
        "sec",
        split_axis=0,
        concat_axis=0,
        tiled=True,
    )
    product, gram_part = products(arrived.reshape(owners * capacity, feature_len), corner)
    gram = total_over_sec(gram_part, owners)
    returned = lax.all_to_all(
        product.reshape(owners, capacity, feature_len),
        "sec",
        split_axis=0,
        concat_axis=0,
        tiled=True,
    )
    home_rows = returned.reshape(owners * capacity, feature_len)[slot_index]
    return solve_rows(gram, home_rows, factor)


def solution(mesh):
    placed = (
        P(("runs", "sec"), None),
        P(("runs", "sec"), None),
        P("runs", None),
        P(("runs", "sec")),
        P(("runs", "sec")),
    )
    return jax.shard_map(
        per_device, mesh=mesh, in_specs=placed, out_specs=P(("runs", "sec"), None), check_vma=False
    )
```

```python
import math

import jax
import jax.numpy as jnp
from jax import lax
from jax.experimental import pallas as pl
from jax.experimental.pallas import tpu as pltpu
from jax.sharding import PartitionSpec as P

B = 128
S = 32
F32 = jnp.float32
BF16 = jnp.bfloat16


def split2(x):
    hi = x.astype(BF16)
    lo = (x - hi.astype(F32)).astype(BF16)
    return hi, lo


def starts(nb):
    offs, at = [], 0
    for j in range(nb):
        offs.append(at)
        at += (nb - j) * B
    return offs, at


def dot(a, b, dims):
    return lax.dot_general(a, b, (dims, ((), ())), preferred_element_type=F32)


def product_kernel(nb, rows_ref, corner_ref, image_ref, gram_ref):
    image = dot(rows_ref[...], corner_ref[...], ((1,), (0,)))
    image_ref[...] = image
    hi, lo = split2(image)
    left = jnp.concatenate([hi, hi, lo], axis=0).T
    right = jnp.concatenate([hi, lo, hi], axis=0)
    offs, _ = starts(nb)
    for j in range(nb):
        gram_ref[pl.ds(offs[j], (nb - j) * B), :] = dot(
            left[j * B :, :], right[:, j * B : (j + 1) * B], ((1,), (0,))
        )


def factor_block(t_ref):
    row8 = lax.broadcasted_iota(jnp.int32, (S, B), 0)
    lane = lax.broadcasted_iota(jnp.int32, (S, B), 1)
    rowb = lax.broadcasted_iota(jnp.int32, (B, 2 * B), 0)

    def step(i, carry):
        at = pl.multiple_of(i * S, S)
        v0 = t_ref[pl.ds(at, S), :B]
        v1 = t_ref[pl.ds(at, S), B:]
        turned = pltpu.roll(v0, lax.rem(B - at, B), 1)
        cols = [jnp.broadcast_to(turned[:, m : m + 1], (S, B)) for m in range(S)]
        scale = jnp.zeros((S, B), F32)
        for j in range(S):
            pivot = cols[j][j : j + 1, :]
            f = jnp.where(row8 > j, cols[j] * (1.0 / pivot), 0.0)
            scale = jnp.where(row8 == j, lax.rsqrt(pivot), scale)
            for m in range(j + 1, S):
                cols[m] = cols[m] - f * cols[m][j : j + 1, :]
            v0 = v0 - f * v0[j : j + 1, :]
            v1 = v1 - f * v1[j : j + 1, :]
        v0 = v0 * scale
        v1 = v1 * scale
        u = jnp.where(lane >= at + S, v0, 0.0)
        uh = u.astype(BF16).astype(F32)
        um = (u - uh).astype(BF16).astype(F32)
        ul = u - uh - um
        v = jnp.concatenate([v0, v1], axis=1)
        vh = v.astype(BF16).astype(F32)
        vm = (v - vh).astype(BF16).astype(F32)
        vl = v - vh - vm
        lhs = jnp.concatenate([uh, uh, um, um, uh, ul], axis=0).astype(BF16)
        rhs = jnp.concatenate([vh, vm, vh, vm, vl, vh], axis=0).astype(BF16)
        change = dot(lhs, rhs, ((0,), (0,)))
        t_ref[...] = t_ref[...] - change
        t_ref[pl.ds(at, S), B:] = v1
        return carry

    lax.fori_loop(0, B // S, step, 0)


def solve_kernel(nb, factor, gram_ref, home_ref, out_ref, a_ref, t_ref):
    offs, total = starts(nb)
    rows = home_ref.shape[0]
    a_ref[...] = gram_ref[...]
    out_ref[...] = home_ref[...]
    eye = (
        lax.broadcasted_iota(jnp.int32, (B, B), 0) == lax.broadcasted_iota(jnp.int32, (B, B), 1)
    ).astype(F32)
    for k in range(nb):
        t_ref[:, :B] = a_ref[pl.ds(offs[k], B), :]
        t_ref[:, B:] = eye
        factor_block(t_ref)
        ih, il = split2(t_ref[:, B:])
        inv = jnp.concatenate([ih, il, ih], axis=1)
        below = (nb - k - 1) * B
        x = out_ref[:, k * B : (k + 1) * B]
        if below:
            x = jnp.concatenate([a_ref[pl.ds(offs[k] + B, below), :], x], axis=0)
        xh, xl = split2(x)
        panel = dot(jnp.concatenate([xh, xh, xl], axis=1), inv, ((1,), (1,)))
        out_ref[:, k * B : (k + 1) * B] = panel[below:, :] * factor
        if below:
            ph, plo = split2(panel)
            left = jnp.concatenate([ph, ph, plo], axis=1)
            right = jnp.concatenate([ph, plo, ph], axis=1)
            for j in range(k + 1, nb):
                at = (j - k - 1) * B
                change = dot(left[at:, :], right[at : at + B, :], ((1,), (1,)))
                size = (nb - j) * B
                a_ref[pl.ds(offs[j], size), :] = a_ref[pl.ds(offs[j], size), :] - change[:size, :]
                out_ref[:, j * B : (j + 1) * B] = (
                    out_ref[:, j * B : (j + 1) * B] - change[size:, :]
                )


def total_kernel(stages, chunks, part_ref, out_ref, acc_ref, inbox_ref, send_sem, recv_sem):
    me = lax.axis_index("sec")
    rows = part_ref.shape[0] // chunks
    bit = [(me // (1 << s)) % 2 for s in range(stages)]
    peer = [me + (1 << s) * (1 - 2 * bit[s]) for s in range(stages)]
    barrier = pltpu.get_barrier_semaphore()
    for s in range(stages):
        pl.semaphore_signal(
            barrier, inc=1, device_id={"sec": peer[s]}, device_id_type=pl.DeviceIdType.MESH
        )
    pl.semaphore_wait(barrier, stages)

    base = [[None] * (stages + 1) for _ in range(chunks)]
    for c in range(chunks):
        base[c][0] = c * rows
        for s in range(stages):
            base[c][s + 1] = base[c][s] + bit[s] * (rows >> (s + 1))

    def window(c, s, flip):
        size = rows >> (s + 1)
        side = 1 - bit[s] if flip else bit[s]
        return pl.ds(pl.multiple_of(base[c][s] + side * size, 8), size)

    def box(c, s):
        return pl.ds(c * rows + rows - (rows >> s), rows >> (s + 1))

    def make(c, t):
        if t < stages:
            source = part_ref if t == 0 else acc_ref
            src = source.at[window(c, t, True), :]
            dst = inbox_ref.at[box(c, t), :]
            s = t
        else:
            s = 2 * stages - 1 - t
            src = out_ref.at[window(c, s, False), :]
            dst = out_ref.at[window(c, s, False), :]
        return pltpu.make_async_remote_copy(
            src_ref=src,
            dst_ref=dst,
            send_sem=send_sem.at[c, t],
            recv_sem=recv_sem.at[c, t],
            device_id={"sec": peer[s]},
            device_id_type=pl.DeviceIdType.MESH,
        )

    copies = {}
    for step in range(2 * stages + chunks):
        for c in range(chunks):
            t = step - c
            if t < 0 or t > 2 * stages:
                continue
            if t > 0:
                copies[c, t - 1].wait()
                if t <= stages:
                    mine = window(c, t - 1, False)
                    source = part_ref if t == 1 else acc_ref
                    result = out_ref if t == stages else acc_ref
                    result[mine, :] = source[mine, :] + inbox_ref[box(c, t - 1), :]
            if t < 2 * stages:
                copies[c, t] = make(c, t)
                copies[c, t].start()


def total_over_sec(part, owners):
    stages = owners.bit_length() - 1
    grain = 8 * owners
    chunks = 4 if part.shape[0] % (4 * grain) == 0 else 1
    rows = -(-part.shape[0] // grain) * grain
    padded = jnp.pad(part, ((0, rows - part.shape[0]), (0, 0)))
    vmem = pl.BlockSpec(memory_space=pltpu.VMEM)
    total = pl.pallas_call(
        lambda *refs: total_kernel(stages, chunks, *refs),
        out_shape=jax.ShapeDtypeStruct((rows, B), F32),
        in_specs=[vmem],
        out_specs=vmem,
        scratch_shapes=[
            pltpu.VMEM((rows, B), F32),
            pltpu.VMEM((rows, B), F32),
            pltpu.SemaphoreType.DMA((chunks, 2 * stages)),
            pltpu.SemaphoreType.DMA((chunks, 2 * stages)),
        ],
        compiler_params=pltpu.CompilerParams(
            collective_id=0, has_side_effects=True, vmem_limit_bytes=40 << 20
        ),
        name="total_over_sec",
    )(padded)
    return total[: part.shape[0]]


def products(rows, corner):
    nb = corner.shape[1] // B
    _, total = starts(nb)
    vmem = pl.BlockSpec(memory_space=pltpu.VMEM)
    return pl.pallas_call(
        lambda *refs: product_kernel(nb, *refs),
        out_shape=(
            jax.ShapeDtypeStruct((rows.shape[0], corner.shape[1]), F32),
            jax.ShapeDtypeStruct((total, B), F32),
        ),
        in_specs=[vmem, vmem],
        out_specs=(vmem, vmem),
        compiler_params=pltpu.CompilerParams(vmem_limit_bytes=48 << 20),
        name="products",
    )(rows, corner)


def solve_rows(gram, home, factor):
    nb = home.shape[1] // B
    vmem = pl.BlockSpec(memory_space=pltpu.VMEM)
    return pl.pallas_call(
        lambda *refs: solve_kernel(nb, factor, *refs),
        out_shape=jax.ShapeDtypeStruct(home.shape, F32),
        in_specs=[vmem, vmem],
        out_specs=vmem,
        scratch_shapes=[pltpu.VMEM(gram.shape, F32), pltpu.VMEM((B, 2 * B), F32)],
        compiler_params=pltpu.CompilerParams(vmem_limit_bytes=48 << 20),
        name="solve_rows",
    )(gram, home)


def per_device(edge_rows, corner, joining, charge_left, charge_right):
    row_count, feature_len = edge_rows.shape
    owners = lax.axis_size("sec")
    capacity = 2 * row_count // owners
    factor = math.sqrt(row_count * owners)
    target = joining[charge_left, charge_right]
    labels = jnp.arange(owners, dtype=jnp.int32)
    onehot = (target[:, None] == labels[None, :]).astype(jnp.int32)
    before = jnp.cumsum(onehot, axis=0) - onehot
    order_in = jnp.sum(before * onehot, axis=1)
    slot_index = target * capacity + order_in
    packed = (
        jnp.zeros((owners * capacity, feature_len), edge_rows.dtype).at[slot_index].set(edge_rows)
    )
    arrived = lax.all_to_all(
        packed.reshape(owners, capacity, feature_len),
        "sec",
        split_axis=0,
        concat_axis=0,
        tiled=True,
    )
    product, gram_part = products(arrived.reshape(owners * capacity, feature_len), corner)
    gram = total_over_sec(gram_part, owners)
    returned = lax.all_to_all(
        product.reshape(owners, capacity, feature_len),
        "sec",
        split_axis=0,
        concat_axis=0,
        tiled=True,
    )
    home_rows = returned.reshape(owners * capacity, feature_len)[slot_index]
    return solve_rows(gram, home_rows, factor)


def solution(mesh):
    placed = (
        P(("runs", "sec"), None),
        P(("runs", "sec"), None),
        P("runs", None),
        P(("runs", "sec")),
        P(("runs", "sec")),
    )
    return jax.shard_map(
        per_device, mesh=mesh, in_specs=placed, out_specs=P(("runs", "sec"), None), check_vma=False
    )
```

```python
import math

import jax
import jax.numpy as jnp
from jax import lax
from jax.experimental import pallas as pl
from jax.experimental.pallas import tpu as pltpu
from jax.sharding import PartitionSpec as P

B = 128
S = 32
F32 = jnp.float32
BF16 = jnp.bfloat16


def split2(x):
    hi = x.astype(BF16)
    lo = (x - hi.astype(F32)).astype(BF16)
    return hi, lo


def starts(nb):
    offs, at = [], 0
    for j in range(nb):
        offs.append(at)
        at += (nb - j) * B
    return offs, at


def dot(a, b, dims):
    return lax.dot_general(a, b, (dims, ((), ())), preferred_element_type=F32)


def product_kernel(nb, rows_ref, corner_ref, image_ref, gram_ref):
    image = dot(rows_ref[...], corner_ref[...], ((1,), (0,)))
    image_ref[...] = image
    hi, lo = split2(image)
    left = jnp.concatenate([hi, hi, lo], axis=0).T
    right = jnp.concatenate([hi, lo, hi], axis=0)
    offs, _ = starts(nb)
    for j in range(nb):
        gram_ref[pl.ds(offs[j], (nb - j) * B), :] = dot(
            left[j * B :, :], right[:, j * B : (j + 1) * B], ((1,), (0,))
        )


def factor_block(t_ref):
    row8 = lax.broadcasted_iota(jnp.int32, (S, B), 0)
    lane = lax.broadcasted_iota(jnp.int32, (S, B), 1)
    rowb = lax.broadcasted_iota(jnp.int32, (B, 2 * B), 0)

    def step(i, carry):
        at = pl.multiple_of(i * S, S)
        v0 = t_ref[pl.ds(at, S), :B]
        v1 = t_ref[pl.ds(at, S), B:]
        turned = pltpu.roll(v0, lax.rem(B - at, B), 1)
        cols = [jnp.broadcast_to(turned[:, m : m + 1], (S, B)) for m in range(S)]
        scale = jnp.zeros((S, B), F32)
        for j in range(S):
            pivot = cols[j][j : j + 1, :]
            f = jnp.where(row8 > j, cols[j] * (1.0 / pivot), 0.0)
            scale = jnp.where(row8 == j, lax.rsqrt(pivot), scale)
            for m in range(j + 1, S):
                cols[m] = cols[m] - f * cols[m][j : j + 1, :]
            v0 = v0 - f * v0[j : j + 1, :]
            v1 = v1 - f * v1[j : j + 1, :]
        v0 = v0 * scale
        v1 = v1 * scale
        u = jnp.where(lane >= at + S, v0, 0.0)
        uh = u.astype(BF16).astype(F32)
        um = (u - uh).astype(BF16).astype(F32)
        ul = u - uh - um
        v = jnp.concatenate([v0, v1], axis=1)
        vh = v.astype(BF16).astype(F32)
        vm = (v - vh).astype(BF16).astype(F32)
        vl = v - vh - vm
        lhs = jnp.concatenate([uh, uh, um, um, uh, ul], axis=0).astype(BF16)
        rhs = jnp.concatenate([vh, vm, vh, vm, vl, vh], axis=0).astype(BF16)
        change = dot(lhs, rhs, ((0,), (0,)))
        t_ref[...] = t_ref[...] - change
        t_ref[pl.ds(at, S), B:] = v1
        return carry

    lax.fori_loop(0, B // S, step, 0)


def factor_kernel(nb, gram_ref, low_ref, t_ref):
    offs, _ = starts(nb)
    low_ref[...] = gram_ref[...]
    eye = (
        lax.broadcasted_iota(jnp.int32, (B, B), 0) == lax.broadcasted_iota(jnp.int32, (B, B), 1)
    ).astype(F32)
    for k in range(nb):
        t_ref[:, :B] = low_ref[pl.ds(offs[k], B), :]
        t_ref[:, B:] = eye
        factor_block(t_ref)
        low_ref[pl.ds(offs[k], B), :] = t_ref[:, B:]
        below = (nb - k - 1) * B
        if below:
            ih, il = split2(t_ref[:, B:])
            xh, xl = split2(low_ref[pl.ds(offs[k] + B, below), :])
            panel = dot(
                jnp.concatenate([xh, xh, xl], axis=1),
                jnp.concatenate([ih, il, ih], axis=1),
                ((1,), (1,)),
            )
            low_ref[pl.ds(offs[k] + B, below), :] = panel
            ph, plo = split2(panel)
            left = jnp.concatenate([ph, ph, plo], axis=1)
            right = jnp.concatenate([ph, plo, ph], axis=1)
            for j in range(k + 1, nb):
                at = (j - k - 1) * B
                change = dot(left[at:, :], right[at : at + B, :], ((1,), (1,)))
                here = pl.ds(offs[j], (nb - j) * B)
                low_ref[here, :] = low_ref[here, :] - change


def apply_kernel(nb, factor, low_ref, home_ref, out_ref):
    offs, _ = starts(nb)
    rest = home_ref[...]
    for k in range(nb):
        ih, il = split2(low_ref[pl.ds(offs[k], B), :])
        xh, xl = split2(rest[:, :B])
        x = dot(
            jnp.concatenate([xh, xh, xl], axis=1),
            jnp.concatenate([ih, il, ih], axis=1),
            ((1,), (1,)),
        )
        out_ref[:, k * B : (k + 1) * B] = x * factor
        below = (nb - k - 1) * B
        if below:
            ph, plo = split2(low_ref[pl.ds(offs[k] + B, below), :])
            xh, xl = split2(x)
            rest = rest[:, B:] - dot(
                jnp.concatenate([xh, xh, xl], axis=1),
                jnp.concatenate([ph, plo, ph], axis=1),
                ((1,), (1,)),
            )


def total_kernel(stages, chunks, part_ref, out_ref, acc_ref, inbox_ref, send_sem, recv_sem):
    me = lax.axis_index("sec")
    rows = part_ref.shape[0] // chunks
    bit = [(me // (1 << s)) % 2 for s in range(stages)]
    peer = [me + (1 << s) * (1 - 2 * bit[s]) for s in range(stages)]
    barrier = pltpu.get_barrier_semaphore()
    for s in range(stages):
        pl.semaphore_signal(
            barrier, inc=1, device_id={"sec": peer[s]}, device_id_type=pl.DeviceIdType.MESH
        )
    pl.semaphore_wait(barrier, stages)

    base = [[None] * (stages + 1) for _ in range(chunks)]
    for c in range(chunks):
        base[c][0] = c * rows
        for s in range(stages):
            base[c][s + 1] = base[c][s] + bit[s] * (rows >> (s + 1))

    def window(c, s, flip):
        size = rows >> (s + 1)
        side = 1 - bit[s] if flip else bit[s]
        return pl.ds(pl.multiple_of(base[c][s] + side * size, 8), size)

    def box(c, s):
        return pl.ds(c * rows + rows - (rows >> s), rows >> (s + 1))

    def make(c, t):
        if t < stages:
            source = part_ref if t == 0 else acc_ref
            src = source.at[window(c, t, True), :]
            dst = inbox_ref.at[box(c, t), :]
            s = t
        else:
            s = 2 * stages - 1 - t
            src = out_ref.at[window(c, s, False), :]
            dst = out_ref.at[window(c, s, False), :]
        return pltpu.make_async_remote_copy(
            src_ref=src,
            dst_ref=dst,
            send_sem=send_sem.at[c, t],
            recv_sem=recv_sem.at[c, t],
            device_id={"sec": peer[s]},
            device_id_type=pl.DeviceIdType.MESH,
        )

    copies = {}
    for step in range(2 * stages + chunks):
        for c in range(chunks):
            t = step - c
            if t < 0 or t > 2 * stages:
                continue
            if t > 0:
                copies[c, t - 1].wait()
                if t <= stages:
                    mine = window(c, t - 1, False)
                    source = part_ref if t == 1 else acc_ref
                    result = out_ref if t == stages else acc_ref
                    result[mine, :] = source[mine, :] + inbox_ref[box(c, t - 1), :]
            if t < 2 * stages:
                copies[c, t] = make(c, t)
                copies[c, t].start()


def total_over_sec(part, owners):
    stages = owners.bit_length() - 1
    grain = 8 * owners
    chunks = 4 if part.shape[0] % (4 * grain) == 0 else 1
    rows = -(-part.shape[0] // grain) * grain
    padded = jnp.pad(part, ((0, rows - part.shape[0]), (0, 0)))
    vmem = pl.BlockSpec(memory_space=pltpu.VMEM)
    total = pl.pallas_call(
        lambda *refs: total_kernel(stages, chunks, *refs),
        out_shape=jax.ShapeDtypeStruct((rows, B), F32),
        in_specs=[vmem],
        out_specs=vmem,
        scratch_shapes=[
            pltpu.VMEM((rows, B), F32),
            pltpu.VMEM((rows, B), F32),
            pltpu.SemaphoreType.DMA((chunks, 2 * stages)),
            pltpu.SemaphoreType.DMA((chunks, 2 * stages)),
        ],
        compiler_params=pltpu.CompilerParams(
            collective_id=0, has_side_effects=True, vmem_limit_bytes=40 << 20
        ),
        name="total_over_sec",
    )(padded)
    return total[: part.shape[0]]


def products(rows, corner):
    nb = corner.shape[1] // B
    _, total = starts(nb)
    vmem = pl.BlockSpec(memory_space=pltpu.VMEM)
    return pl.pallas_call(
        lambda *refs: product_kernel(nb, *refs),
        out_shape=(
            jax.ShapeDtypeStruct((rows.shape[0], corner.shape[1]), F32),
            jax.ShapeDtypeStruct((total, B), F32),
        ),
        in_specs=[vmem, vmem],
        out_specs=(vmem, vmem),
        compiler_params=pltpu.CompilerParams(vmem_limit_bytes=48 << 20),
        name="products",
    )(rows, corner)


def factor_gram(gram):
    nb = int((2 * gram.shape[0] // B) ** 0.5)
    vmem = pl.BlockSpec(memory_space=pltpu.VMEM)
    return pl.pallas_call(
        lambda *refs: factor_kernel(nb, *refs),
        out_shape=jax.ShapeDtypeStruct(gram.shape, F32),
        in_specs=[vmem],
        out_specs=vmem,
        scratch_shapes=[pltpu.VMEM((B, 2 * B), F32)],
        compiler_params=pltpu.CompilerParams(vmem_limit_bytes=40 << 20),
        cost_estimate=pl.CostEstimate(
            flops=30_000_000_000, bytes_accessed=80_000_000, transcendentals=0
        ),
        name="factor_gram",
    )(gram)


def apply_factor(low, home, factor):
    nb = home.shape[1] // B
    vmem = pl.BlockSpec(memory_space=pltpu.VMEM)
    return pl.pallas_call(
        lambda *refs: apply_kernel(nb, factor, *refs),
        out_shape=jax.ShapeDtypeStruct(home.shape, F32),
        in_specs=[vmem, vmem],
        out_specs=vmem,
        compiler_params=pltpu.CompilerParams(vmem_limit_bytes=40 << 20),
        name="apply_factor",
    )(low, home)


def per_device(edge_rows, corner, joining, charge_left, charge_right):
    row_count, feature_len = edge_rows.shape
    owners = lax.axis_size("sec")
    capacity = 2 * row_count // owners
    factor = math.sqrt(row_count * owners)
    target = joining[charge_left, charge_right]
    labels = jnp.arange(owners, dtype=jnp.int32)
    onehot = (target[:, None] == labels[None, :]).astype(jnp.int32)
    before = jnp.cumsum(onehot, axis=0) - onehot
    order_in = jnp.sum(before * onehot, axis=1)
    slot_index = target * capacity + order_in
    packed = (
        jnp.zeros((owners * capacity, feature_len), edge_rows.dtype).at[slot_index].set(edge_rows)
    )
    arrived = lax.all_to_all(
        packed.reshape(owners, capacity, feature_len),
        "sec",
        split_axis=0,
        concat_axis=0,
        tiled=True,
    )
    product, gram_part = products(arrived.reshape(owners * capacity, feature_len), corner)
    gram = total_over_sec(gram_part, owners)
    gram, product = lax.optimization_barrier((gram, product))
    returned = lax.all_to_all(
        product.reshape(owners, capacity, feature_len),
        "sec",
        split_axis=0,
        concat_axis=0,
        tiled=True,
    )
    home_rows = returned.reshape(owners * capacity, feature_len)[slot_index]
    return apply_factor(factor_gram(gram), home_rows, factor)


def solution(mesh):
    placed = (
        P(("runs", "sec"), None),
        P(("runs", "sec"), None),
        P("runs", None),
        P(("runs", "sec")),
        P(("runs", "sec")),
    )
    return jax.shard_map(
        per_device, mesh=mesh, in_specs=placed, out_specs=P(("runs", "sec"), None), check_vma=False
    )
```

```python
import math

import jax
import jax.numpy as jnp
from jax import lax
from jax.experimental import pallas as pl
from jax.experimental.pallas import tpu as pltpu
from jax.sharding import PartitionSpec as P

B = 128
S = 32
F32 = jnp.float32
BF16 = jnp.bfloat16


def split2(x):
    hi = x.astype(BF16)
    lo = (x - hi.astype(F32)).astype(BF16)
    return hi, lo


def starts(nb):
    offs, at = [], 0
    for j in range(nb):
        offs.append(at)
        at += (nb - j) * B
    return offs, at


def dot(a, b, dims):
    return lax.dot_general(a, b, (dims, ((), ())), preferred_element_type=F32)


def product_kernel(nb, rows_ref, corner_ref, image_ref, gram_ref):
    image = dot(rows_ref[...], corner_ref[...], ((1,), (0,)))
    image_ref[...] = image
    hi, lo = split2(image)
    left = jnp.concatenate([hi, hi, lo], axis=0).T
    right = jnp.concatenate([hi, lo, hi], axis=0)
    offs, _ = starts(nb)
    for j in range(nb):
        gram_ref[pl.ds(offs[j], (nb - j) * B), :] = dot(
            left[j * B :, :], right[:, j * B : (j + 1) * B], ((1,), (0,))
        )


def factor_block(t_ref):
    row8 = lax.broadcasted_iota(jnp.int32, (S, B), 0)
    lane = lax.broadcasted_iota(jnp.int32, (S, B), 1)
    rowb = lax.broadcasted_iota(jnp.int32, (B, 2 * B), 0)

    def step(i, carry):
        at = pl.multiple_of(i * S, S)
        v0 = t_ref[pl.ds(at, S), :B]
        v1 = t_ref[pl.ds(at, S), B:]
        turned = pltpu.roll(v0, lax.rem(B - at, B), 1)
        cols = [jnp.broadcast_to(turned[:, m : m + 1], (S, B)) for m in range(S)]
        scale = jnp.zeros((S, B), F32)
        for j in range(S):
            pivot = cols[j][j : j + 1, :]
            f = jnp.where(row8 > j, cols[j] * (1.0 / pivot), 0.0)
            scale = jnp.where(row8 == j, lax.rsqrt(pivot), scale)
            for m in range(j + 1, S):
                cols[m] = cols[m] - f * cols[m][j : j + 1, :]
            v0 = v0 - f * v0[j : j + 1, :]
            v1 = v1 - f * v1[j : j + 1, :]
        v0 = v0 * scale
        v1 = v1 * scale
        u = jnp.where(lane >= at + S, v0, 0.0)
        uh = u.astype(BF16).astype(F32)
        um = (u - uh).astype(BF16).astype(F32)
        ul = u - uh - um
        v = jnp.concatenate([v0, v1], axis=1)
        vh = v.astype(BF16).astype(F32)
        vm = (v - vh).astype(BF16).astype(F32)
        vl = v - vh - vm
        lhs = jnp.concatenate([uh, uh, um, um, uh, ul], axis=0).astype(BF16)
        rhs = jnp.concatenate([vh, vm, vh, vm, vl, vh], axis=0).astype(BF16)
        change = dot(lhs, rhs, ((0,), (0,)))
        t_ref[...] = t_ref[...] - change
        t_ref[pl.ds(at, S), B:] = v1
        return carry

    lax.fori_loop(0, B // S, step, 0)


def factor_kernel(nb, gram_ref, low_ref, t_ref):
    offs, _ = starts(nb)
    low_ref[...] = gram_ref[...]
    eye = (
        lax.broadcasted_iota(jnp.int32, (B, B), 0) == lax.broadcasted_iota(jnp.int32, (B, B), 1)
    ).astype(F32)
    for k in range(nb):
        t_ref[:, :B] = low_ref[pl.ds(offs[k], B), :]
        t_ref[:, B:] = eye
        factor_block(t_ref)
        low_ref[pl.ds(offs[k], B), :] = t_ref[:, B:]
        below = (nb - k - 1) * B
        if below:
            ih, il = split2(t_ref[:, B:])
            xh, xl = split2(low_ref[pl.ds(offs[k] + B, below), :])
            panel = dot(
                jnp.concatenate([xh, xh, xl], axis=1),
                jnp.concatenate([ih, il, ih], axis=1),
                ((1,), (1,)),
            )
            low_ref[pl.ds(offs[k] + B, below), :] = panel
            ph, plo = split2(panel)
            left = jnp.concatenate([ph, ph, plo], axis=1)
            right = jnp.concatenate([ph, plo, ph], axis=1)
            for j in range(k + 1, nb):
                at = (j - k - 1) * B
                change = dot(left[at:, :], right[at : at + B, :], ((1,), (1,)))
                here = pl.ds(offs[j], (nb - j) * B)
                low_ref[here, :] = low_ref[here, :] - change


def hot(index, count):
    lane = lax.broadcasted_iota(jnp.int32, (index.shape[0], count), 1)
    return (lane == index).astype(F32)


def apply_kernel(nb, factor, low_ref, back_ref, slot_ref, out_ref):
    offs, _ = starts(nb)
    back = back_ref[...]
    pick = hot(slot_ref[...], back.shape[0]).astype(BF16)
    hi = back.astype(BF16)
    mid, lo = split2(back - hi.astype(F32))
    rest = dot(pick, hi, ((1,), (0,))) + (
        dot(pick, mid, ((1,), (0,))) + dot(pick, lo, ((1,), (0,)))
    )
    for k in range(nb):
        ih, il = split2(low_ref[pl.ds(offs[k], B), :])
        xh, xl = split2(rest[:, :B])
        x = dot(
            jnp.concatenate([xh, xh, xl], axis=1),
            jnp.concatenate([ih, il, ih], axis=1),
            ((1,), (1,)),
        )
        out_ref[:, k * B : (k + 1) * B] = x * factor
        below = (nb - k - 1) * B
        if below:
            ph, plo = split2(low_ref[pl.ds(offs[k] + B, below), :])
            xh, xl = split2(x)
            rest = rest[:, B:] - dot(
                jnp.concatenate([xh, xh, xl], axis=1),
                jnp.concatenate([ph, plo, ph], axis=1),
                ((1,), (1,)),
            )


def total_kernel(stages, chunks, part_ref, out_ref, acc_ref, inbox_ref, send_sem, recv_sem):
    me = lax.axis_index("sec")
    rows = part_ref.shape[0] // chunks
    bit = [(me // (1 << s)) % 2 for s in range(stages)]
    peer = [me + (1 << s) * (1 - 2 * bit[s]) for s in range(stages)]
    barrier = pltpu.get_barrier_semaphore()
    for s in range(stages):
        pl.semaphore_signal(
            barrier, inc=1, device_id={"sec": peer[s]}, device_id_type=pl.DeviceIdType.MESH
        )
    pl.semaphore_wait(barrier, stages)

    base = [[None] * (stages + 1) for _ in range(chunks)]
    for c in range(chunks):
        base[c][0] = c * rows
        for s in range(stages):
            base[c][s + 1] = base[c][s] + bit[s] * (rows >> (s + 1))

    def window(c, s, flip):
        size = rows >> (s + 1)
        side = 1 - bit[s] if flip else bit[s]
        return pl.ds(pl.multiple_of(base[c][s] + side * size, 8), size)

    def box(c, s):
        return pl.ds(c * rows + rows - (rows >> s), rows >> (s + 1))

    def make(c, t):
        if t < stages:
            source = part_ref if t == 0 else acc_ref
            src = source.at[window(c, t, True), :]
            dst = inbox_ref.at[box(c, t), :]
            s = t
        else:
            s = 2 * stages - 1 - t
            src = out_ref.at[window(c, s, False), :]
            dst = out_ref.at[window(c, s, False), :]
        return pltpu.make_async_remote_copy(
            src_ref=src,
            dst_ref=dst,
            send_sem=send_sem.at[c, t],
            recv_sem=recv_sem.at[c, t],
            device_id={"sec": peer[s]},
            device_id_type=pl.DeviceIdType.MESH,
        )

    copies = {}
    for step in range(2 * stages + chunks):
        for c in range(chunks):
            t = step - c
            if t < 0 or t > 2 * stages:
                continue
            if t > 0:
                copies[c, t - 1].wait()
                if t <= stages:
                    mine = window(c, t - 1, False)
                    source = part_ref if t == 1 else acc_ref
                    result = out_ref if t == stages else acc_ref
                    result[mine, :] = source[mine, :] + inbox_ref[box(c, t - 1), :]
            if t < 2 * stages:
                copies[c, t] = make(c, t)
                copies[c, t].start()


def total_over_sec(part, owners):
    stages = owners.bit_length() - 1
    grain = 8 * owners
    chunks = 6 if part.shape[0] % (6 * grain) == 0 else 1
    rows = -(-part.shape[0] // grain) * grain
    padded = jnp.pad(part, ((0, rows - part.shape[0]), (0, 0)))
    vmem = pl.BlockSpec(memory_space=pltpu.VMEM)
    total = pl.pallas_call(
        lambda *refs: total_kernel(stages, chunks, *refs),
        out_shape=jax.ShapeDtypeStruct((rows, B), F32),
        in_specs=[vmem],
        out_specs=vmem,
        scratch_shapes=[
            pltpu.VMEM((rows, B), F32),
            pltpu.VMEM((rows, B), F32),
            pltpu.SemaphoreType.DMA((chunks, 2 * stages)),
            pltpu.SemaphoreType.DMA((chunks, 2 * stages)),
        ],
        compiler_params=pltpu.CompilerParams(
            collective_id=0, has_side_effects=True, vmem_limit_bytes=20 << 20
        ),
        name="total_over_sec",
    )(padded)
    return total[: part.shape[0]]


def products(rows, corner):
    nb = corner.shape[1] // B
    _, total = starts(nb)
    vmem = pl.BlockSpec(memory_space=pltpu.VMEM)
    return pl.pallas_call(
        lambda *refs: product_kernel(nb, *refs),
        out_shape=(
            jax.ShapeDtypeStruct((rows.shape[0], corner.shape[1]), F32),
            jax.ShapeDtypeStruct((total, B), F32),
        ),
        in_specs=[vmem, vmem],
        out_specs=(vmem, vmem),
        compiler_params=pltpu.CompilerParams(vmem_limit_bytes=20 << 20),
        name="products",
    )(rows, corner)


def factor_gram(gram):
    nb = int((2 * gram.shape[0] // B) ** 0.5)
    vmem = pl.BlockSpec(memory_space=pltpu.VMEM)
    return pl.pallas_call(
        lambda *refs: factor_kernel(nb, *refs),
        out_shape=jax.ShapeDtypeStruct(gram.shape, F32),
        in_specs=[vmem],
        out_specs=vmem,
        scratch_shapes=[pltpu.VMEM((B, 2 * B), F32)],
        compiler_params=pltpu.CompilerParams(vmem_limit_bytes=20 << 20),
        cost_estimate=pl.CostEstimate(
            flops=30_000_000_000, bytes_accessed=80_000_000, transcendentals=0
        ),
        name="factor_gram",
    )(gram)


def apply_factor(low, back, slot, factor):
    nb = back.shape[1] // B
    vmem = pl.BlockSpec(memory_space=pltpu.VMEM)
    return pl.pallas_call(
        lambda *refs: apply_kernel(nb, factor, *refs),
        out_shape=jax.ShapeDtypeStruct((slot.shape[0], back.shape[1]), F32),
        in_specs=[vmem, vmem, vmem],
        out_specs=vmem,
        compiler_params=pltpu.CompilerParams(vmem_limit_bytes=20 << 20),
        name="apply_factor",
    )(low, back, slot)


def route_kernel(capacity, edge_ref, joining_ref, left_ref, right_ref, packed_ref, slot_ref):
    rows = edge_ref.shape[0]
    owners = joining_ref.shape[0]
    table = joining_ref[...].astype(F32).astype(BF16)
    picked = dot(hot(left_ref[...], owners).astype(BF16), table, ((1,), (0,)))
    target = jnp.sum(picked * hot(right_ref[...], owners), axis=1, keepdims=True)
    mine = hot(target.astype(jnp.int32), owners)
    earlier = (
        lax.broadcasted_iota(jnp.int32, (rows, rows), 0)
        > lax.broadcasted_iota(jnp.int32, (rows, rows), 1)
    ).astype(F32)
    before = dot(earlier.astype(BF16), mine.astype(BF16), ((1,), (0,)))
    order = jnp.sum(before * mine, axis=1, keepdims=True)
    slot = (target * capacity + order).astype(jnp.int32)
    slot_ref[...] = slot
    place = hot(slot, packed_ref.shape[0]).astype(BF16)
    packed_ref[...] = dot(place, edge_ref[...], ((0,), (0,))).astype(packed_ref.dtype)


def route(edge_rows, joining, charge_left, charge_right, capacity):
    rows, feature_len = edge_rows.shape
    vmem = pl.BlockSpec(memory_space=pltpu.VMEM)
    return pl.pallas_call(
        lambda *refs: route_kernel(capacity, *refs),
        out_shape=(
            jax.ShapeDtypeStruct((joining.shape[0] * capacity, feature_len), edge_rows.dtype),
            jax.ShapeDtypeStruct((rows, 1), jnp.int32),
        ),
        in_specs=[vmem] * 4,
        out_specs=(vmem, vmem),
        name="route",
    )(edge_rows, joining, charge_left[:, None], charge_right[:, None])


def per_device(edge_rows, corner, joining, charge_left, charge_right):
    row_count, feature_len = edge_rows.shape
    owners = lax.axis_size("sec")
    capacity = 2 * row_count // owners
    factor = math.sqrt(row_count * owners)
    packed, slot = route(edge_rows, joining, charge_left, charge_right, capacity)
    arrived = lax.all_to_all(
        packed.reshape(owners, capacity, feature_len),
        "sec",
        split_axis=0,
        concat_axis=0,
        tiled=True,
    )
    product, gram_part = products(arrived.reshape(owners * capacity, feature_len), corner)
    gram = total_over_sec(gram_part, owners)
    gram, product = lax.optimization_barrier((gram, product))
    returned = lax.all_to_all(
        product.reshape(owners, capacity, feature_len),
        "sec",
        split_axis=0,
        concat_axis=0,
        tiled=True,
    )
    back = returned.reshape(owners * capacity, feature_len)
    return apply_factor(factor_gram(gram), back, slot, factor)


def solution(mesh):
    placed = (
        P(("runs", "sec"), None),
        P(("runs", "sec"), None),
        P("runs", None),
        P(("runs", "sec")),
        P(("runs", "sec")),
    )
    return jax.shard_map(
        per_device, mesh=mesh, in_specs=placed, out_specs=P(("runs", "sec"), None), check_vma=False
    )
```

```python
import math

import jax
import jax.numpy as jnp
from jax import lax
from jax.experimental import pallas as pl
from jax.experimental.pallas import tpu as pltpu
from jax.sharding import PartitionSpec as P

B = 128
S = 32
F32 = jnp.float32
BF16 = jnp.bfloat16


def split2(x):
    hi = x.astype(BF16)
    lo = (x - hi.astype(F32)).astype(BF16)
    return hi, lo


def starts(nb):
    offs, at = [], 0
    for j in range(nb):
        offs.append(at)
        at += (nb - j) * B
    return offs, at


def dot(a, b, dims):
    return lax.dot_general(a, b, (dims, ((), ())), preferred_element_type=F32)


def product_kernel(nb, rows_ref, corner_ref, image_ref, gram_ref):
    image = dot(rows_ref[...], corner_ref[...], ((1,), (0,)))
    image_ref[...] = image
    hi, lo = split2(image)
    left = jnp.concatenate([hi, hi, lo], axis=0).T
    right = jnp.concatenate([hi, lo, hi], axis=0)
    offs, _ = starts(nb)
    for j in range(nb):
        gram_ref[pl.ds(offs[j], (nb - j) * B), :] = dot(
            left[j * B :, :], right[:, j * B : (j + 1) * B], ((1,), (0,))
        )


def factor_block(t_ref):
    row8 = lax.broadcasted_iota(jnp.int32, (S, B), 0)
    lane = lax.broadcasted_iota(jnp.int32, (S, B), 1)
    rowb = lax.broadcasted_iota(jnp.int32, (B, 2 * B), 0)

    def step(i, carry):
        at = pl.multiple_of(i * S, S)
        v0 = t_ref[pl.ds(at, S), :B]
        v1 = t_ref[pl.ds(at, S), B:]
        turned = pltpu.roll(v0, lax.rem(B - at, B), 1)
        cols = [jnp.broadcast_to(turned[:, m : m + 1], (S, B)) for m in range(S)]
        scale = jnp.zeros((S, B), F32)
        for j in range(S):
            pivot = cols[j][j : j + 1, :]
            f = jnp.where(row8 > j, cols[j] * (1.0 / pivot), 0.0)
            scale = jnp.where(row8 == j, lax.rsqrt(pivot), scale)
            for m in range(j + 1, S):
                cols[m] = cols[m] - f * cols[m][j : j + 1, :]
            v0 = v0 - f * v0[j : j + 1, :]
            v1 = v1 - f * v1[j : j + 1, :]
        v0 = v0 * scale
        v1 = v1 * scale
        u = jnp.where(lane >= at + S, v0, 0.0)
        uh = u.astype(BF16).astype(F32)
        um = (u - uh).astype(BF16).astype(F32)
        ul = u - uh - um
        v = jnp.concatenate([v0, v1], axis=1)
        vh = v.astype(BF16).astype(F32)
        vm = (v - vh).astype(BF16).astype(F32)
        vl = v - vh - vm
        lhs = jnp.concatenate([uh, uh, um, um, uh, ul], axis=0).astype(BF16)
        rhs = jnp.concatenate([vh, vm, vh, vm, vl, vh], axis=0).astype(BF16)
        change = dot(lhs, rhs, ((0,), (0,)))
        t_ref[...] = t_ref[...] - change
        t_ref[pl.ds(at, S), B:] = v1
        return carry

    lax.fori_loop(0, B // S, step, 0)


def factor_kernel(nb, gram_ref, low_ref, t_ref):
    offs, _ = starts(nb)
    low_ref[...] = gram_ref[...]
    eye = (
        lax.broadcasted_iota(jnp.int32, (B, B), 0) == lax.broadcasted_iota(jnp.int32, (B, B), 1)
    ).astype(F32)
    for k in range(nb):
        t_ref[:, :B] = low_ref[pl.ds(offs[k], B), :]
        t_ref[:, B:] = eye
        factor_block(t_ref)
        low_ref[pl.ds(offs[k], B), :] = t_ref[:, B:]
        below = (nb - k - 1) * B
        if below:
            ih, il = split2(t_ref[:, B:])
            xh, xl = split2(low_ref[pl.ds(offs[k] + B, below), :])
            panel = dot(
                jnp.concatenate([xh, xh, xl], axis=1),
                jnp.concatenate([ih, il, ih], axis=1),
                ((1,), (1,)),
            )
            low_ref[pl.ds(offs[k] + B, below), :] = panel
            ph, plo = split2(panel)
            left = jnp.concatenate([ph, ph, plo], axis=1)
            right = jnp.concatenate([ph, plo, ph], axis=1)
            for j in range(k + 1, nb):
                at = (j - k - 1) * B
                change = dot(left[at:, :], right[at : at + B, :], ((1,), (1,)))
                here = pl.ds(offs[j], (nb - j) * B)
                low_ref[here, :] = low_ref[here, :] - change


def hot(index, count):
    row = lax.broadcasted_iota(jnp.int32, (count, index.shape[1]), 0)
    return (row == index).astype(F32)


def apply_kernel(nb, factor, low_any, back_ref, slot_ref, out_ref, low_ref, sem):
    copy = pltpu.make_async_copy(low_any, low_ref, sem)
    copy.start()
    offs, _ = starts(nb)
    back = back_ref[...]
    pick = hot(slot_ref[...], back.shape[0]).astype(BF16)
    hi = back.astype(BF16)
    mid, lo = split2(back - hi.astype(F32))
    rest = dot(pick, hi, ((0,), (0,))) + (
        dot(pick, mid, ((0,), (0,))) + dot(pick, lo, ((0,), (0,)))
    )
    copy.wait()
    for k in range(nb):
        ih, il = split2(low_ref[pl.ds(offs[k], B), :])
        xh, xl = split2(rest[:, :B])
        x = dot(
            jnp.concatenate([xh, xh, xl], axis=1),
            jnp.concatenate([ih, il, ih], axis=1),
            ((1,), (1,)),
        )
        out_ref[:, k * B : (k + 1) * B] = x * factor
        below = (nb - k - 1) * B
        if below:
            ph, plo = split2(low_ref[pl.ds(offs[k] + B, below), :])
            xh, xl = split2(x)
            rest = rest[:, B:] - dot(
                jnp.concatenate([xh, xh, xl], axis=1),
                jnp.concatenate([ph, plo, ph], axis=1),
                ((1,), (1,)),
            )


def total_kernel(stages, chunks, part_ref, out_ref, acc_ref, inbox_ref, send_sem, recv_sem):
    me = lax.axis_index("sec")
    rows = part_ref.shape[0] // chunks
    bit = [(me // (1 << s)) % 2 for s in range(stages)]
    peer = [me + (1 << s) * (1 - 2 * bit[s]) for s in range(stages)]
    barrier = pltpu.get_barrier_semaphore()
    for s in range(stages):
        pl.semaphore_signal(
            barrier, inc=1, device_id={"sec": peer[s]}, device_id_type=pl.DeviceIdType.MESH
        )
    pl.semaphore_wait(barrier, stages)

    base = [[None] * (stages + 1) for _ in range(chunks)]
    for c in range(chunks):
        base[c][0] = c * rows
        for s in range(stages):
            base[c][s + 1] = base[c][s] + bit[s] * (rows >> (s + 1))

    def window(c, s, flip):
        size = rows >> (s + 1)
        side = 1 - bit[s] if flip else bit[s]
        return pl.ds(pl.multiple_of(base[c][s] + side * size, 8), size)

    def box(c, s):
        return pl.ds(c * rows + rows - (rows >> s), rows >> (s + 1))

    def make(c, t):
        if t < stages:
            source = part_ref if t == 0 else acc_ref
            src = source.at[window(c, t, True), :]
            dst = inbox_ref.at[box(c, t), :]
            s = t
        else:
            s = 2 * stages - 1 - t
            src = out_ref.at[window(c, s, False), :]
            dst = out_ref.at[window(c, s, False), :]
        return pltpu.make_async_remote_copy(
            src_ref=src,
            dst_ref=dst,
            send_sem=send_sem.at[c, t],
            recv_sem=recv_sem.at[c, t],
            device_id={"sec": peer[s]},
            device_id_type=pl.DeviceIdType.MESH,
        )

    copies = {}
    for step in range(2 * stages + chunks):
        for c in range(chunks):
            t = step - c
            if t < 0 or t > 2 * stages:
                continue
            if t > 0:
                copies[c, t - 1].wait()
                if t <= stages:
                    mine = window(c, t - 1, False)
                    source = part_ref if t == 1 else acc_ref
                    result = out_ref if t == stages else acc_ref
                    result[mine, :] = source[mine, :] + inbox_ref[box(c, t - 1), :]
            if t < 2 * stages:
                copies[c, t] = make(c, t)
                copies[c, t].start()


def total_over_sec(part, owners):
    stages = owners.bit_length() - 1
    grain = 8 * owners
    chunks = 3 if part.shape[0] % (3 * grain) == 0 else 1
    rows = -(-part.shape[0] // grain) * grain
    padded = jnp.pad(part, ((0, rows - part.shape[0]), (0, 0)))
    vmem = pl.BlockSpec(memory_space=pltpu.VMEM)
    total = pl.pallas_call(
        lambda *refs: total_kernel(stages, chunks, *refs),
        out_shape=jax.ShapeDtypeStruct((rows, B), F32),
        in_specs=[vmem],
        out_specs=vmem,
        scratch_shapes=[
            pltpu.VMEM((rows, B), F32),
            pltpu.VMEM((rows, B), F32),
            pltpu.SemaphoreType.DMA((chunks, 2 * stages)),
            pltpu.SemaphoreType.DMA((chunks, 2 * stages)),
        ],
        compiler_params=pltpu.CompilerParams(
            collective_id=0, has_side_effects=True, vmem_limit_bytes=20 << 20
        ),
        name="total_over_sec",
    )(padded)
    return total[: part.shape[0]]


def products(rows, corner):
    nb = corner.shape[1] // B
    _, total = starts(nb)
    vmem = pl.BlockSpec(memory_space=pltpu.VMEM)
    return pl.pallas_call(
        lambda *refs: product_kernel(nb, *refs),
        out_shape=(
            jax.ShapeDtypeStruct((rows.shape[0], corner.shape[1]), F32),
            jax.ShapeDtypeStruct((total, B), F32),
        ),
        in_specs=[vmem, vmem],
        out_specs=(vmem, vmem),
        compiler_params=pltpu.CompilerParams(vmem_limit_bytes=20 << 20),
        name="products",
    )(rows, corner)


def factor_gram(gram):
    nb = int((2 * gram.shape[0] // B) ** 0.5)
    vmem = pl.BlockSpec(memory_space=pltpu.VMEM)
    return pl.pallas_call(
        lambda *refs: factor_kernel(nb, *refs),
        out_shape=jax.ShapeDtypeStruct(gram.shape, F32),
        in_specs=[vmem],
        out_specs=vmem,
        scratch_shapes=[pltpu.VMEM((B, 2 * B), F32)],
        compiler_params=pltpu.CompilerParams(vmem_limit_bytes=20 << 20),
        cost_estimate=pl.CostEstimate(
            flops=30_000_000_000, bytes_accessed=80_000_000, transcendentals=0
        ),
        name="factor_gram",
    )(gram)


def apply_factor(low, back, slot, factor):
    nb = back.shape[1] // B
    vmem = pl.BlockSpec(memory_space=pltpu.VMEM)
    return pl.pallas_call(
        lambda *refs: apply_kernel(nb, factor, *refs),
        out_shape=jax.ShapeDtypeStruct((slot.shape[1], back.shape[1]), F32),
        in_specs=[pl.BlockSpec(memory_space=pl.ANY), vmem, vmem],
        out_specs=vmem,
        scratch_shapes=[pltpu.VMEM(low.shape, F32), pltpu.SemaphoreType.DMA],
        compiler_params=pltpu.CompilerParams(vmem_limit_bytes=20 << 20),
        name="apply_factor",
    )(low, back, slot)


def route_kernel(capacity, edge_ref, joining_ref, left_ref, right_ref, packed_ref, slot_ref):
    rows = edge_ref.shape[0]
    owners = joining_ref.shape[0]
    table = joining_ref[...].astype(F32).astype(BF16)
    picked = dot(table, hot(left_ref[...], owners).astype(BF16), ((0,), (0,)))
    target = jnp.sum(picked * hot(right_ref[...], owners), axis=0, keepdims=True)
    mine = hot(target.astype(jnp.int32), owners)
    earlier = (
        lax.broadcasted_iota(jnp.int32, (rows, rows), 0)
        < lax.broadcasted_iota(jnp.int32, (rows, rows), 1)
    ).astype(F32)
    before = dot(mine.astype(BF16), earlier.astype(BF16), ((1,), (0,)))
    order = jnp.sum(before * mine, axis=0, keepdims=True)
    slot = (target * capacity + order).astype(jnp.int32)
    slot_ref[...] = slot
    place = hot(slot, packed_ref.shape[0]).astype(BF16)
    packed_ref[...] = dot(place, edge_ref[...], ((1,), (0,))).astype(packed_ref.dtype)


def route(edge_rows, joining, charge_left, charge_right, capacity):
    rows, feature_len = edge_rows.shape
    vmem = pl.BlockSpec(memory_space=pltpu.VMEM)
    return pl.pallas_call(
        lambda *refs: route_kernel(capacity, *refs),
        out_shape=(
            jax.ShapeDtypeStruct((joining.shape[0] * capacity, feature_len), edge_rows.dtype),
            jax.ShapeDtypeStruct((1, rows), jnp.int32),
        ),
        in_specs=[vmem] * 4,
        out_specs=(vmem, vmem),
        name="route",
    )(edge_rows, joining, charge_left[None, :], charge_right[None, :])


def per_device(edge_rows, corner, joining, charge_left, charge_right):
    row_count, feature_len = edge_rows.shape
    owners = lax.axis_size("sec")
    capacity = 2 * row_count // owners
    factor = math.sqrt(row_count * owners)
    packed, slot = route(edge_rows, joining, charge_left, charge_right, capacity)
    arrived = lax.all_to_all(
        packed.reshape(owners, capacity, feature_len),
        "sec",
        split_axis=0,
        concat_axis=0,
        tiled=True,
    )
    product, gram_part = products(arrived.reshape(owners * capacity, feature_len), corner)
    gram = total_over_sec(gram_part, owners)
    gram, product = lax.optimization_barrier((gram, product))
    returned = lax.all_to_all(
        product.reshape(owners, capacity, feature_len),
        "sec",
        split_axis=0,
        concat_axis=0,
        tiled=True,
    )
    back = returned.reshape(owners * capacity, feature_len)
    return apply_factor(factor_gram(gram), back, slot, factor)


def solution(mesh):
    placed = (
        P(("runs", "sec"), None),
        P(("runs", "sec"), None),
        P("runs", None),
        P(("runs", "sec")),
        P(("runs", "sec")),
    )
    return jax.shard_map(
        per_device, mesh=mesh, in_specs=placed, out_specs=P(("runs", "sec"), None), check_vma=False
    )
```

```python
import math

import jax
import jax.numpy as jnp
from jax import lax
from jax.experimental import pallas as pl
from jax.experimental.pallas import tpu as pltpu
from jax.sharding import PartitionSpec as P

B = 128
S = 32
F32 = jnp.float32
BF16 = jnp.bfloat16


def split2(x):
    hi = x.astype(BF16)
    lo = (x - hi.astype(F32)).astype(BF16)
    return hi, lo


def starts(nb):
    offs, at = [], 0
    for j in range(nb):
        offs.append(at)
        at += (nb - j) * B
    return offs, at


def dot(a, b, dims):
    return lax.dot_general(a, b, (dims, ((), ())), preferred_element_type=F32)


def product_kernel(nb, rows_ref, corner_ref, image_ref, gram_ref):
    image = dot(rows_ref[...], corner_ref[...], ((1,), (0,)))
    image_ref[...] = image
    hi, lo = split2(image)
    left = jnp.concatenate([hi, hi, lo], axis=0).T
    right = jnp.concatenate([hi, lo, hi], axis=0)
    offs, _ = starts(nb)
    for j in range(nb):
        gram_ref[pl.ds(offs[j], (nb - j) * B), :] = dot(
            left[j * B :, :], right[:, j * B : (j + 1) * B], ((1,), (0,))
        )


def factor_block(t_ref):
    row8 = lax.broadcasted_iota(jnp.int32, (S, B), 0)
    lane = lax.broadcasted_iota(jnp.int32, (S, B), 1)
    rowb = lax.broadcasted_iota(jnp.int32, (B, 2 * B), 0)

    def step(i, carry):
        at = pl.multiple_of(i * S, S)
        v0 = t_ref[pl.ds(at, S), :B]
        v1 = t_ref[pl.ds(at, S), B:]
        turned = pltpu.roll(v0, lax.rem(B - at, B), 1)
        cols = [jnp.broadcast_to(turned[:, m : m + 1], (S, B)) for m in range(S)]
        scale = jnp.zeros((S, B), F32)
        for j in range(S):
            pivot = cols[j][j : j + 1, :]
            f = jnp.where(row8 > j, cols[j] * (1.0 / pivot), 0.0)
            scale = jnp.where(row8 == j, lax.rsqrt(pivot), scale)
            for m in range(j + 1, S):
                cols[m] = cols[m] - f * cols[m][j : j + 1, :]
            v0 = v0 - f * v0[j : j + 1, :]
            v1 = v1 - f * v1[j : j + 1, :]
        v0 = v0 * scale
        v1 = v1 * scale
        u = jnp.where(lane >= at + S, v0, 0.0)
        uh = u.astype(BF16).astype(F32)
        um = (u - uh).astype(BF16).astype(F32)
        ul = u - uh - um
        v = jnp.concatenate([v0, v1], axis=1)
        vh = v.astype(BF16).astype(F32)
        vm = (v - vh).astype(BF16).astype(F32)
        vl = v - vh - vm
        lhs = jnp.concatenate([uh, uh, um, um, uh, ul], axis=0).astype(BF16)
        rhs = jnp.concatenate([vh, vm, vh, vm, vl, vh], axis=0).astype(BF16)
        change = dot(lhs, rhs, ((0,), (0,)))
        t_ref[...] = t_ref[...] - change
        t_ref[pl.ds(at, S), B:] = v1
        return carry

    lax.fori_loop(0, B // S, step, 0)


def factor_kernel(nb, gram_ref, low_ref, t_ref):
    offs, _ = starts(nb)
    low_ref[...] = gram_ref[...]
    eye = (
        lax.broadcasted_iota(jnp.int32, (B, B), 0) == lax.broadcasted_iota(jnp.int32, (B, B), 1)
    ).astype(F32)
    for k in range(nb):
        t_ref[:, :B] = low_ref[pl.ds(offs[k], B), :]
        t_ref[:, B:] = eye
        factor_block(t_ref)
        low_ref[pl.ds(offs[k], B), :] = t_ref[:, B:]
        below = (nb - k - 1) * B
        if below:
            ih, il = split2(t_ref[:, B:])
            xh, xl = split2(low_ref[pl.ds(offs[k] + B, below), :])
            panel = dot(
                jnp.concatenate([xh, xh, xl], axis=1),
                jnp.concatenate([ih, il, ih], axis=1),
                ((1,), (1,)),
            )
            low_ref[pl.ds(offs[k] + B, below), :] = panel
            ph, plo = split2(panel)
            left = jnp.concatenate([ph, ph, plo], axis=1)
            right = jnp.concatenate([ph, plo, ph], axis=1)
            for j in range(k + 1, nb):
                at = (j - k - 1) * B
                change = dot(left[at:, :], right[at : at + B, :], ((1,), (1,)))
                here = pl.ds(offs[j], (nb - j) * B)
                low_ref[here, :] = low_ref[here, :] - change


def hot(index, count):
    row = lax.broadcasted_iota(jnp.int32, (count, index.shape[1]), 0)
    return (row == index).astype(F32)


def apply_kernel(nb, factor, low_any, back_ref, slot_ref, out_ref, low_ref, sem):
    copy = pltpu.make_async_copy(low_any, low_ref, sem)
    copy.start()
    offs, _ = starts(nb)
    back = back_ref[...]
    pick = hot(slot_ref[...], back.shape[0]).astype(BF16)
    hi = back.astype(BF16)
    mid, lo = split2(back - hi.astype(F32))
    rest = dot(pick, hi, ((0,), (0,))) + (
        dot(pick, mid, ((0,), (0,))) + dot(pick, lo, ((0,), (0,)))
    )
    copy.wait()
    for k in range(nb):
        ih, il = split2(low_ref[pl.ds(offs[k], B), :])
        xh, xl = split2(rest[:, :B])
        x = dot(
            jnp.concatenate([xh, xh, xl], axis=1),
            jnp.concatenate([ih, il, ih], axis=1),
            ((1,), (1,)),
        )
        out_ref[:, k * B : (k + 1) * B] = x * factor
        below = (nb - k - 1) * B
        if below:
            ph, plo = split2(low_ref[pl.ds(offs[k] + B, below), :])
            xh, xl = split2(x)
            rest = rest[:, B:] - dot(
                jnp.concatenate([xh, xh, xl], axis=1),
                jnp.concatenate([ph, plo, ph], axis=1),
                ((1,), (1,)),
            )


def total_kernel(stages, chunks, part_ref, out_ref, acc_ref, inbox_ref, send_sem, recv_sem):
    me = lax.axis_index("sec")
    rows = part_ref.shape[0] // chunks
    bit = [(me // (1 << s)) % 2 for s in range(stages)]
    peer = [me + (1 << s) * (1 - 2 * bit[s]) for s in range(stages)]
    barrier = pltpu.get_barrier_semaphore()
    for s in range(stages):
        pl.semaphore_signal(
            barrier, inc=1, device_id={"sec": peer[s]}, device_id_type=pl.DeviceIdType.MESH
        )
    pl.semaphore_wait(barrier, stages)

    base = [[None] * (stages + 1) for _ in range(chunks)]
    for c in range(chunks):
        base[c][0] = c * rows
        for s in range(stages):
            base[c][s + 1] = base[c][s] + bit[s] * (rows >> (s + 1))

    def window(c, s, flip):
        size = rows >> (s + 1)
        side = 1 - bit[s] if flip else bit[s]
        return pl.ds(pl.multiple_of(base[c][s] + side * size, 8), size)

    def box(c, s):
        return pl.ds(c * rows + rows - (rows >> s), rows >> (s + 1))

    def make(c, t):
        if t < stages:
            source = part_ref if t == 0 else acc_ref
            src = source.at[window(c, t, True), :]
            dst = inbox_ref.at[box(c, t), :]
            s = t
        else:
            s = 2 * stages - 1 - t
            src = out_ref.at[window(c, s, False), :]
            dst = out_ref.at[window(c, s, False), :]
        return pltpu.make_async_remote_copy(
            src_ref=src,
            dst_ref=dst,
            send_sem=send_sem.at[c, t],
            recv_sem=recv_sem.at[c, t],
            device_id={"sec": peer[s]},
            device_id_type=pl.DeviceIdType.MESH,
        )

    copies = {}
    for step in range(2 * stages + chunks):
        for c in range(chunks):
            t = step - c
            if t < 0 or t > 2 * stages:
                continue
            if t > 0:
                copies[c, t - 1].wait()
                if t <= stages:
                    mine = window(c, t - 1, False)
                    source = part_ref if t == 1 else acc_ref
                    result = out_ref if t == stages else acc_ref
                    result[mine, :] = source[mine, :] + inbox_ref[box(c, t - 1), :]
            if t < 2 * stages:
                copies[c, t] = make(c, t)
                copies[c, t].start()


def total_over_sec(part, owners):
    stages = owners.bit_length() - 1
    grain = 8 * owners
    chunks = 4 if part.shape[0] % (4 * grain) == 0 else 1
    rows = -(-part.shape[0] // grain) * grain
    padded = jnp.pad(part, ((0, rows - part.shape[0]), (0, 0)))
    vmem = pl.BlockSpec(memory_space=pltpu.VMEM)
    total = pl.pallas_call(
        lambda *refs: total_kernel(stages, chunks, *refs),
        out_shape=jax.ShapeDtypeStruct((rows, B), F32),
        in_specs=[vmem],
        out_specs=vmem,
        scratch_shapes=[
            pltpu.VMEM((rows, B), F32),
            pltpu.VMEM((rows, B), F32),
            pltpu.SemaphoreType.DMA((chunks, 2 * stages)),
            pltpu.SemaphoreType.DMA((chunks, 2 * stages)),
        ],
        compiler_params=pltpu.CompilerParams(
            collective_id=0, has_side_effects=True, vmem_limit_bytes=40 << 20
        ),
        name="total_over_sec",
    )(padded)
    return total[: part.shape[0]]


def products(rows, corner):
    nb = corner.shape[1] // B
    _, total = starts(nb)
    vmem = pl.BlockSpec(memory_space=pltpu.VMEM)
    return pl.pallas_call(
        lambda *refs: product_kernel(nb, *refs),
        out_shape=(
            jax.ShapeDtypeStruct((rows.shape[0], corner.shape[1]), F32),
            jax.ShapeDtypeStruct((total, B), F32),
        ),
        in_specs=[vmem, vmem],
        out_specs=(vmem, vmem),
        compiler_params=pltpu.CompilerParams(vmem_limit_bytes=48 << 20),
        name="products",
    )(rows, corner)


def factor_gram(gram):
    nb = int((2 * gram.shape[0] // B) ** 0.5)
    vmem = pl.BlockSpec(memory_space=pltpu.VMEM)
    return pl.pallas_call(
        lambda *refs: factor_kernel(nb, *refs),
        out_shape=jax.ShapeDtypeStruct(gram.shape, F32),
        in_specs=[vmem],
        out_specs=vmem,
        scratch_shapes=[pltpu.VMEM((B, 2 * B), F32)],
        compiler_params=pltpu.CompilerParams(vmem_limit_bytes=40 << 20),
        cost_estimate=pl.CostEstimate(
            flops=30_000_000_000, bytes_accessed=80_000_000, transcendentals=0
        ),
        name="factor_gram",
    )(gram)


def apply_factor(low, back, slot, factor):
    nb = back.shape[1] // B
    vmem = pl.BlockSpec(memory_space=pltpu.VMEM)
    return pl.pallas_call(
        lambda *refs: apply_kernel(nb, factor, *refs),
        out_shape=jax.ShapeDtypeStruct((slot.shape[1], back.shape[1]), F32),
        in_specs=[pl.BlockSpec(memory_space=pl.ANY), vmem, vmem],
        out_specs=vmem,
        scratch_shapes=[pltpu.VMEM(low.shape, F32), pltpu.SemaphoreType.DMA],
        compiler_params=pltpu.CompilerParams(vmem_limit_bytes=40 << 20),
        name="apply_factor",
    )(low, back, slot)


def route_kernel(capacity, edge_ref, joining_ref, left_ref, right_ref, packed_ref, slot_ref):
    rows = edge_ref.shape[0]
    owners = joining_ref.shape[0]
    table = joining_ref[...].astype(F32).astype(BF16)
    picked = dot(table, hot(left_ref[...], owners).astype(BF16), ((0,), (0,)))
    target = jnp.sum(picked * hot(right_ref[...], owners), axis=0, keepdims=True)
    mine = hot(target.astype(jnp.int32), owners)
    earlier = (
        lax.broadcasted_iota(jnp.int32, (rows, rows), 0)
        < lax.broadcasted_iota(jnp.int32, (rows, rows), 1)
    ).astype(F32)
    before = dot(mine.astype(BF16), earlier.astype(BF16), ((1,), (0,)))
    order = jnp.sum(before * mine, axis=0, keepdims=True)
    slot = (target * capacity + order).astype(jnp.int32)
    slot_ref[...] = slot
    place = hot(slot, packed_ref.shape[0]).astype(BF16)
    packed_ref[...] = dot(place, edge_ref[...], ((1,), (0,))).astype(packed_ref.dtype)


def route(edge_rows, joining, charge_left, charge_right, capacity):
    rows, feature_len = edge_rows.shape
    vmem = pl.BlockSpec(memory_space=pltpu.VMEM)
    return pl.pallas_call(
        lambda *refs: route_kernel(capacity, *refs),
        out_shape=(
            jax.ShapeDtypeStruct((joining.shape[0] * capacity, feature_len), edge_rows.dtype),
            jax.ShapeDtypeStruct((1, rows), jnp.int32),
        ),
        in_specs=[vmem] * 4,
        out_specs=(vmem, vmem),
        name="route",
    )(edge_rows, joining, charge_left[None, :], charge_right[None, :])


def per_device(edge_rows, corner, joining, charge_left, charge_right):
    row_count, feature_len = edge_rows.shape
    owners = lax.axis_size("sec")
    capacity = 2 * row_count // owners
    factor = math.sqrt(row_count * owners)
    packed, slot = route(edge_rows, joining, charge_left, charge_right, capacity)
    arrived = lax.all_to_all(
        packed.reshape(owners, capacity, feature_len),
        "sec",
        split_axis=0,
        concat_axis=0,
        tiled=True,
    )
    product, gram_part = products(arrived.reshape(owners * capacity, feature_len), corner)
    gram = total_over_sec(gram_part, owners)
    gram, product = lax.optimization_barrier((gram, product))
    returned = lax.all_to_all(
        product.reshape(owners, capacity, feature_len),
        "sec",
        split_axis=0,
        concat_axis=0,
        tiled=True,
    )
    back = returned.reshape(owners * capacity, feature_len)
    return apply_factor(factor_gram(gram), back, slot, factor)


def solution(mesh):
    placed = (
        P(("runs", "sec"), None),
        P(("runs", "sec"), None),
        P("runs", None),
        P(("runs", "sec")),
        P(("runs", "sec")),
    )
    return jax.shard_map(
        per_device, mesh=mesh, in_specs=placed, out_specs=P(("runs", "sec"), None), check_vma=False
    )
```
